32 devices in a mesh: section: 2 (over x), dp: 16 (over z, y, core).
Axes of the slice: x: 2, y: 2, z: 4, core: 2. Of those that a mesh axis runs over, the one named last changes fastest.
Arguments:
- edge_data: bfloat16 [2, 2, 1024, 960], P('section', None, 'dp'), may hold values from -6 to 6
- segment_ids: int32 [2, 1024], P(None, 'dp'), may hold values from 0 to 63, as said below
- attn_weight: bfloat16 [2, 960, 2560], P('section', None, 'dp'), may hold values from -0.1875 to 0.1875
- ffn_weight: bfloat16 [2, 3, 960, 2560], P('section', None, None, 'dp'), may hold values from -0.1875 to 0.1875
- gains: bfloat16 [2, 1920], P('section', 'dp'), may hold values from 0.5 to 1.5
Outputs:
- edge_out: bfloat16 [2, 2, 1024, 960], P('section', None, 'dp')
- attention_grad: float32 [2, 960, 2560], P('section', None, 'dp')
- ffn_grad: float32 [2, 3, 960, 2560], P('section', None, None, 'dp')
- gain_grad: float32 [2, 1920], P('section', 'dp')
The draws below stay inside these ranges and needn't reach their ends.
Inputs may be any that keep to these rules, and one draw needn't show every extreme that they name: `segment_ids`: inside each aligned block of 64 tokens (one index of dp in one micro-batch) the ids start at 0 at the block's first token and rise by 0 or 1 from token to token; tokens of a block with equal ids form one sequence; no sequence crosses a block; some sequence fills a whole block, and some block holds only sequences of one token.
All inputs are finite; a program needn't handle non-finite values.
Results may differ from the reference program's by a relative error of at most 0.02.
Values may be sent and summed in bfloat16 or wider, within the bound.
No kernel may reach another device: no remote copies, remote signals or barrier semaphores. Data moves between devices by JAX's collectives and lax.ppermute only.
A program may use at most 256 MiB of HBM per device.

```python
import jax
import jax.numpy as jnp
from jax import lax

D = 960
QUERY_HEADS = 15
KEY_VALUE_HEADS = 5
HEAD_SIZE = 64
FF = 2560
ATTN_COLS = 2560
MB = 2
TOK_DEV = 64
TOKENS = 1024
N_DP = 16


def draw_segment_ids(key, part):
    block_count = TOKENS // TOK_DEV
    rate_key, flag_key = jax.random.split(key)
    span_table = jnp.array([1, 2, 4, 8, 16, 32], dtype=jnp.int32)
    rate_pick = jax.random.randint(rate_key, (MB, block_count, 1), 0, 6)
    start_odds = span_table[rate_pick]
    draw_values = jax.random.randint(flag_key, (MB, block_count, TOK_DEV), 0, 64)
    position = jnp.arange(TOK_DEV, dtype=jnp.int32)
    start_flags = (draw_values < start_odds) | (position == 0)
    block_number = jnp.arange(MB * block_count, dtype=jnp.int32).reshape(MB, block_count, 1)
    start_flags = start_flags & ((block_number > 0) | (position == 0))
    start_flags = start_flags | (block_number == MB * block_count - 1)
    segment_out = jnp.cumsum(start_flags.astype(jnp.int32), axis=-1) - 1
    return segment_out.reshape(MB, TOKENS)


def steps_of(rng, shape, cuts, smallest, high):
    level = 1.0
    for dim, parts in cuts:
        heights = jax.random.uniform(jax.random.fold_in(jax.random.fold_in(rng, 6), dim), (parts,), jnp.float32, smallest / len(cuts), high / len(cuts))
        level = level * jnp.repeat(jnp.exp(heights), shape[dim] // parts).reshape((-1,) + (1,) * (len(shape) - 1 - dim))
    return level


def centred(key, shape, scale, reach, cuts=(), kind=jnp.bfloat16):
    values = scale * jax.random.normal(key, shape, jnp.float32)
    if cuts:
        values = values * steps_of(key, shape, cuts, -0.22, 0.18)
    return jnp.clip(values, -reach, reach).astype(kind)


def setup_inputs(seed: int = 0) -> dict:
    streams_of = jax.random.split(jax.random.key(seed), 6)
    return {
        "edge_data": centred(streams_of[0], (2, MB, TOKENS, D), 1.0, 6.0, ((0, 2), (2, 16))),
        "segment_ids": draw_segment_ids(jax.random.fold_in(streams_of[5], 71), 0),
        "attn_weight": centred(streams_of[2], (2, D, ATTN_COLS), D ** -0.5, 0.1875, ((0, 2), (2, 16))),
        "ffn_weight": centred(streams_of[3], (2, 3, D, FF), D ** -0.5, 0.1875, ((0, 2), (3, 16))),
        "gains": jnp.clip(1.0 + 0.1 * jax.random.normal(streams_of[4], (2, 2 * D), jnp.float32), 0.5, 1.5).astype(jnp.bfloat16),
    }


@jax.custom_vjp
def lower_half(v):
    return lax.optimization_barrier(v.astype(jnp.bfloat16)).astype(jnp.float32)

@jax.custom_vjp
def low_back(v):
    return v

def low_keep(v):
    return (lower_half(v), None)

def low_pass(kept, grad):
    return (grad,)

def back_keep(v):
    return (v, None)

def back_low(kept, grad):
    return (lower_half(grad),)
lower_half.defvjp(low_keep, low_pass)
low_back.defvjp(back_keep, back_low)
highest = lax.Precision.HIGHEST
epsilon = 1e-05
theta_base = 100000.0

def norm_rows(rows, gain):
    return rows * lax.rsqrt(lax.optimization_barrier(jnp.mean(rows * rows, axis=-1, keepdims=True)) + epsilon) * gain

def rotary_apply(rows, cosine_table, sine_values):
    half_size = rows.shape[-1] // 2
    front_part = rows[..., :half_size]
    back_part = rows[..., half_size:]
    return jnp.concatenate([front_part * cosine_table - back_part * sine_values, back_part * cosine_table + front_part * sine_values], axis=-1)

def block_tables(segments):
    block_len = segments.shape[-1]
    offsets = jnp.arange(block_len, dtype=jnp.int32)
    same_segment = segments[..., :, None] == segments[..., None, :]
    segment_start = lax.optimization_barrier(jnp.min(jnp.where(same_segment, offsets, block_len), axis=-1))
    positions = (offsets - segment_start).astype(jnp.float32)
    half_size = HEAD_SIZE // 2
    frequency = theta_base ** (-(2.0 * jnp.arange(half_size, dtype=jnp.float32)) / HEAD_SIZE)
    angles = positions[..., None] * frequency
    allowed = same_segment & (offsets[:, None] >= offsets[None, :])
    return (jnp.cos(angles), jnp.sin(angles), allowed)

def layer(inputs, attn_w, ffn_w, gain_row, cosine_table, sine_values, allowed):
    batch_rows_count, sequence_length, model_width = inputs.shape
    head_column_width = QUERY_HEADS * HEAD_SIZE
    key_value_width = KEY_VALUE_HEADS * HEAD_SIZE
    query_group_count = QUERY_HEADS // KEY_VALUE_HEADS
    score_scale = HEAD_SIZE ** (-0.5)
    split_at = head_column_width + 2 * key_value_width
    normed = lower_half(norm_rows(inputs, gain_row[:model_width]))
    projected_rows = low_back(jnp.einsum('btd,dc->btc', normed, attn_w[:, :split_at], precision=highest))
    query_matrix = lower_half(rotary_apply(projected_rows[..., :head_column_width].reshape(batch_rows_count, sequence_length, KEY_VALUE_HEADS, query_group_count, HEAD_SIZE), cosine_table[:, :, None, None, :], sine_values[:, :, None, None, :]))
    key_matrix_rows = lower_half(rotary_apply(projected_rows[..., head_column_width:head_column_width + key_value_width].reshape(batch_rows_count, sequence_length, KEY_VALUE_HEADS, HEAD_SIZE), cosine_table[:, :, None, :], sine_values[:, :, None, :]))
    value_matrix_rows = lower_half(projected_rows[..., head_column_width + key_value_width:].reshape(batch_rows_count, sequence_length, KEY_VALUE_HEADS, HEAD_SIZE))
    scores = low_back(score_scale * jnp.einsum('btgrd,bugd->bgrtu', query_matrix, key_matrix_rows, precision=highest))
    masked = jnp.where(allowed[:, None, None], scores, -1000000000.0)
    prob_low = lower_half(jax.nn.softmax(masked, axis=-1))
    attended = jnp.einsum('bgrtu,bugd->btgrd', prob_low, value_matrix_rows, precision=highest).reshape(batch_rows_count, sequence_length, head_column_width)
    attended = low_back(lower_half(attended))
    branch_out = low_back(jnp.einsum('bti,di->btd', attended, attn_w[:, split_at:], precision=highest))
    hidden = inputs + branch_out
    normed_two = lower_half(norm_rows(hidden, gain_row[model_width:]))
    gate_proj = low_back(jnp.einsum('btd,df->btf', normed_two, ffn_w[0], precision=highest))
    upward = low_back(jnp.einsum('btd,df->btf', normed_two, ffn_w[1], precision=highest))
    active = lower_half(jax.nn.silu(gate_proj) * upward)
    return hidden + low_back(jnp.einsum('btf,df->btd', active, ffn_w[2], precision=highest))

def reference(edge_data, segment_ids, attn_weight, ffn_weight, gains):
    block_count = MB * N_DP
    inputs = edge_data[0].astype(jnp.float32).reshape(block_count, TOK_DEV, D)
    cotangent = edge_data[1].astype(jnp.float32).reshape(block_count, TOK_DEV, D)
    cosine_table, sine_values, allowed = block_tables(segment_ids.reshape(block_count, TOK_DEV))

    def forward(first_in, attn_all, ffn_all, gain_all):
        middle = low_back(lower_half(layer(first_in, attn_all[0], ffn_all[0], gain_all[0], cosine_table, sine_values, allowed)))
        return layer(middle, attn_all[1], ffn_all[1], gain_all[1], cosine_table, sine_values, allowed)
    result, pullback = jax.vjp(forward, inputs, attn_weight.astype(jnp.float32), ffn_weight.astype(jnp.float32), gains.astype(jnp.float32))
    input_grad, attention_grad, ffn_grad, gain_grad = pullback(cotangent)
    edge_out = jnp.stack([input_grad.reshape(MB, TOKENS, D), result.reshape(MB, TOKENS, D)]).astype(jnp.bfloat16)
    return (edge_out, attention_grad, ffn_grad, gain_grad)
```

```python
import jax
import jax.numpy as jnp
from jax import lax
from jax.sharding import PartitionSpec as P

QUERY_HEADS = 15
KEY_VALUE_HEADS = 5
GROUP = QUERY_HEADS // KEY_VALUE_HEADS
HEAD_SIZE = 64
BLOCK = 64
QCOLS = QUERY_HEADS * HEAD_SIZE
KVCOLS = KEY_VALUE_HEADS * HEAD_SIZE
SPLIT = QCOLS + 2 * KVCOLS
SCALE = HEAD_SIZE ** (-0.5)
EPS = 1e-05
THETA = 100000.0
BF = jnp.bfloat16
F32 = jnp.float32


def matmul(a, b):
    return jnp.dot(a, b, preferred_element_type=F32)


def right_trans(a, b):
    return lax.dot_general(a, b, (((1,), (1,)), ((), ())), preferred_element_type=F32)


def left_trans(a, b):
    return lax.dot_general(a, b, (((0,), (0,)), ((), ())), preferred_element_type=F32)


def inv_rms(x):
    return lax.rsqrt(jnp.mean(x * x, axis=-1, keepdims=True) + EPS)


def rope(x, cos, sin):
    half = HEAD_SIZE // 2
    a = x[..., :half]
    b = x[..., half:]
    return jnp.concatenate([a * cos - b * sin, b * cos + a * sin], axis=-1)


def tables(segment_ids):
    seg = segment_ids.reshape(-1)
    tokens = seg.shape[0]
    idx = jnp.arange(tokens, dtype=jnp.int32)
    seg = seg + BLOCK * (idx // BLOCK)
    same = seg[:, None] == seg[None, :]
    start = jnp.min(jnp.where(same, idx[None, :], tokens), axis=-1)
    pos = (idx - start).astype(F32)
    half = HEAD_SIZE // 2
    freq = THETA ** (-(2.0 * jnp.arange(half, dtype=F32)) / HEAD_SIZE)
    ang = pos[:, None] * freq
    allowed = same & (idx[:, None] >= idx[None, :])
    return jnp.cos(ang), jnp.sin(ang), allowed


def scores(q, k, allowed):
    s = jnp.einsum("grtd,gud->grtu", q, k, preferred_element_type=F32) * SCALE
    return jnp.where(allowed, s, -1000000000.0)


def forward(u, w, tabs):
    qkv_t, out_t, gate_t, up_t, down_t, g1, g2 = w
    cos, sin, allowed = tabs
    rows = u.shape[0]
    n = (u * inv_rms(u) * g1).astype(BF)
    proj = right_trans(n, qkv_t)
    heads = proj.reshape(rows, -1, HEAD_SIZE).transpose(1, 0, 2)
    turned = rope(heads[: QUERY_HEADS + KEY_VALUE_HEADS], cos, sin).astype(BF)
    q = turned[:QUERY_HEADS].reshape(KEY_VALUE_HEADS, GROUP, rows, HEAD_SIZE)
    k = turned[QUERY_HEADS:]
    v = heads[QUERY_HEADS + KEY_VALUE_HEADS :].astype(BF)
    s = scores(q, k, allowed)
    peak = jnp.max(s, axis=-1, keepdims=True)
    lse = peak + jnp.log(jnp.sum(jnp.exp(s - peak), axis=-1, keepdims=True))
    p = jnp.exp(s - lse).astype(BF)
    o = jnp.einsum("grtu,gud->grtd", p, v, preferred_element_type=F32)
    o = o.astype(BF).reshape(QUERY_HEADS, rows, HEAD_SIZE).transpose(1, 0, 2).reshape(rows, QCOLS)
    h1 = u + matmul(o, out_t)
    m = (h1 * inv_rms(h1) * g2).astype(BF)
    gate = right_trans(m, gate_t)
    up = right_trans(m, up_t)
    act = (gate * jax.nn.sigmoid(gate) * up).astype(BF)
    out = h1 + matmul(act, down_t)
    return out, (u, n, q, k, v, lse, o, h1, m, gate, up, act)


def norm_back(dy, x, g):
    r = inv_rms(x)
    dg = dy * g
    dx = r * dg - x * (r * r * r) * jnp.mean(dg * x, axis=-1, keepdims=True)
    return dx, jnp.sum(dy * x * r, axis=0)


def backward(e, saved, w, tabs):
    u, n, q, k, v, lse, o, h1, m, gate, up, act = saved
    qkv_t, out_t, gate_t, up_t, down_t, g1, g2 = w
    cos, sin, allowed = tabs
    rows = u.shape[0]
    eb = e.astype(BF)
    da = right_trans(eb, down_t)
    sg = jax.nn.sigmoid(gate)
    dgate = (da * up * sg * (1.0 + gate * (1.0 - sg))).astype(BF)
    dup = (da * (gate * sg)).astype(BF)
    dm = matmul(dgate, gate_t) + matmul(dup, up_t)
    dx, gain2 = norm_back(dm, h1, g2)
    dh1 = e + dx
    dz = dh1.astype(BF)
    do = right_trans(dz, out_t).astype(BF)
    do = do.reshape(rows, QUERY_HEADS, HEAD_SIZE).transpose(1, 0, 2)
    do = do.reshape(KEY_VALUE_HEADS, GROUP, rows, HEAD_SIZE)
    p = jnp.exp(scores(q, k, allowed) - lse)
    dv = jnp.einsum("grtu,grtd->gud", p.astype(BF), do, preferred_element_type=F32)
    dp = jnp.einsum("grtd,gud->grtu", do, v, preferred_element_type=F32)
    ds = (p * (dp - jnp.sum(dp * p, axis=-1, keepdims=True))).astype(BF)
    dq = jnp.einsum("grtu,gud->grtd", ds, k, preferred_element_type=F32) * SCALE
    dk = jnp.einsum("grtu,grtd->gud", ds, q, preferred_element_type=F32) * SCALE
    dq = dq.reshape(QUERY_HEADS, rows, HEAD_SIZE)
    dqk = rope(jnp.concatenate([dq, dk], axis=0), cos, -sin)
    dproj = jnp.concatenate([dqk, dv], axis=0).astype(BF).transpose(1, 0, 2).reshape(rows, SPLIT)
    dn = matmul(dproj, qkv_t)
    dx, gain1 = norm_back(dn, u, g1)
    return dh1 + dx, (eb, dgate, dup, dz, dproj), jnp.concatenate([gain1, gain2])


def to_owners(columns, owners):
    rows, cols = columns.shape
    share = cols // owners
    blocks = columns.reshape(rows, owners, share).transpose(1, 0, 2)
    return lax.all_to_all(blocks, "dp", 0, 0, tiled=True).reshape(owners * rows, share)


def local(edge_data, segment_ids, attn_weight, ffn_weight, gains):
    owners = lax.axis_size("dp")
    share = attn_weight.shape[2]
    leading = lax.axis_index("section") == 0

    def whole(x):
        return lax.all_gather(x, "dp", axis=0, tiled=True)

    gain_row = whole(gains[0]).astype(F32)
    attn_t = whole(attn_weight[0].T)
    gate_t = whole(ffn_weight[0, 0].T)
    up_t = whole(ffn_weight[0, 1].T)
    down_t = whole(ffn_weight[0, 2].T)
    width = attn_t.shape[1]
    w = (attn_t[:SPLIT], attn_t[SPLIT:], gate_t, up_t, down_t, gain_row[:width], gain_row[width:])
    tabs = tables(segment_ids)
    edge = edge_data[0].reshape(-1, width)

    first_out, _ = forward(edge.astype(F32), w, tabs)
    received = lax.ppermute(first_out.astype(BF), "section", [(0, 1)])
    layer_in = jnp.where(leading, edge, received).astype(F32)
    out, saved = forward(layer_in, w, tabs)
    n, o, m, act = saved[1], saved[6], saved[8], saved[11]
    n_all = whole(n)
    m_all = whole(m)

    sent, _, _ = backward(edge.astype(F32), saved, w, tabs)
    grad_in = lax.ppermute(sent.astype(BF), "section", [(1, 0)])
    e = jnp.where(leading, grad_in, edge).astype(F32)
    du, (eb, dgate, dup, dz, dproj), gain_part = backward(e, saved, w, tabs)
    eb_all = whole(eb)
    dz_all = whole(dz)

    act_own = to_owners(act, owners)
    gate_own = to_owners(dgate, owners)
    up_own = to_owners(dup, owners)
    attn_own = to_owners(jnp.concatenate([dproj, o], axis=1), owners)
    column = lax.axis_index("dp") * share + jnp.arange(share, dtype=jnp.int32)
    attn_grad = jnp.where(
        column < SPLIT, left_trans(n_all, attn_own), left_trans(dz_all, attn_own)
    )
    ffn_grad = jnp.stack(
        [
            left_trans(m_all, gate_own),
            left_trans(m_all, up_own),
            left_trans(eb_all, act_own),
        ]
    )
    gain_grad = lax.psum_scatter(gain_part, "dp", scatter_dimension=0, tiled=True)
    edge_out = jnp.where(leading, du, out).astype(BF).reshape(edge_data.shape[1:])
    return edge_out[None], attn_grad[None], ffn_grad[None], gain_grad[None]


def solution(mesh):
    in_specs = (
        P("section", None, "dp", None),
        P(None, "dp"),
        P("section", None, "dp"),
        P("section", None, None, "dp"),
        P("section", "dp"),
    )
    out_specs = (
        P("section", None, "dp", None),
        P("section", None, "dp"),
        P("section", None, None, "dp"),
        P("section", "dp"),
    )
    return jax.shard_map(local, mesh=mesh, in_specs=in_specs, out_specs=out_specs, check_vma=False)
```
